32 devices in a mesh: gx: 2 (over x), gy: 4 (over y, core), gz: 4 (over z).
Axes of the slice: x: 2, y: 2, z: 4, core: 2. Of those that a mesh axis runs over, the one named last changes fastest.
Arguments:
- seed_cotangent: bfloat16 [2, 4, 4, 112, 2048], P('gx', 'gy', 'gz'), may hold values from -6 to 6
- trace_operator: bfloat16 [2, 4, 4, 2048, 2048], P('gx', 'gy', 'gz'), may hold values from -0.125 to 0.125
- face_matrices: bfloat16 [2, 4, 4, 6, 340, 340], P('gx', 'gy', 'gz'), may hold values from -0.3125 to 0.3125
- saved_traces: bfloat16 [2, 4, 4, 3, 112, 2048], P('gx', 'gy', 'gz'), may hold values from -6 to 6
- edge_flags: int32 [2, 4, 4, 6], P('gx', 'gy', 'gz'), may hold values 0 or 1
- node_map: int32 [2, 4, 4, 6, 340], P('gx', 'gy', 'gz'), may hold values from 0 to 339, each once within a row
Outputs:
- adjoint_traces: bfloat16 [2, 4, 4, 112, 2048], P('gx', 'gy', 'gz')
- face_gradient: bfloat16 [2, 4, 4, 6, 340, 340], P('gx', 'gy', 'gz')
The draws below stay inside these ranges and needn't reach their ends.
Inputs may be any that keep to these rules, and one draw needn't show every extreme that they name: Each row node_map[.., k, :] names every face node once.
All inputs are finite; a program needn't handle non-finite values. No bound on the sum of `edge_flags` on one device may be relied on, other than what follows from the above.
Results may differ from the reference program's by a relative error of at most 0.0085.
Values may be sent and summed in bfloat16 or wider, within the bound.
A program may use at most 64 MiB of HBM per device.

```python
import jax
import jax.numpy as jnp
from jax import lax

TRACE = 2048
F = 340
COLS = 112
ITERS = 3
NX = 2
NY = 4
NZ = 4


def set_ends(result, own_key, low, top_value):
    longest = result.shape.index(max(result.shape))
    spots = []
    for shift in (0, 1):
        where = [jax.random.randint(jax.random.fold_in(own_key, axis), (), 0, length) for axis, length in enumerate(result.shape)]
        where[longest] = (where[longest] + shift) % result.shape[longest]
        spots.append(tuple(where))
    return result.at[spots[0]].set(low).at[spots[1]].set(top_value)


def level_of(key, shape, split, smallest, largest):
    factor_of = 1.0
    for dim, blocks in split:
        draws = jax.random.uniform(jax.random.fold_in(jax.random.fold_in(key, 6), dim), (blocks,), jnp.float32, smallest / len(split), largest / len(split))
        factor_of = factor_of * jnp.repeat(jnp.exp(draws), shape[dim] // blocks).reshape((-1,) + (1,) * (len(shape) - 1 - dim))
    return factor_of


def scatter_about(rng, dims, deviation, bound, cuts=(), kind=jnp.bfloat16):
    level = level_of(rng, dims, cuts, -0.22, 0.18) if cuts else 1.0
    result = jax.random.normal(rng, dims, jnp.float32) * deviation * level
    return jnp.minimum(jnp.maximum(result, -bound), bound).astype(kind)


def setup_inputs(seed: int = 0) -> dict:
    seeds = jax.random.split(jax.random.key(seed), 7)
    return {
        "seed_cotangent": scatter_about(seeds[0], (NX, NY, NZ, COLS, TRACE), 1.0, 6.0, ((0, 2), (1, 4), (2, 4))),
        "trace_operator": scatter_about(seeds[1], (NX, NY, NZ, TRACE, TRACE), TRACE ** -0.5, 0.125, ((0, 2), (1, 4), (2, 4))),
        "face_matrices": scatter_about(seeds[2], (NX, NY, NZ, 6, F, F), F ** -0.5, 0.3125, ((0, 2), (1, 4), (2, 4))),
        "saved_traces": scatter_about(seeds[3], (NX, NY, NZ, ITERS, COLS, TRACE), 1.0, 6.0, ((0, 2), (1, 4), (2, 4))),
        "edge_flags": set_ends((jax.random.randint(seeds[4], (NX, NY, NZ, 6), 0, 4) < 1).astype(jnp.int32), jax.random.fold_in(seeds[4], 1), 0, 1),
        "node_map": jax.vmap(lambda own: jax.random.permutation(own, F))(jax.random.split(seeds[5], NX * NY * NZ * 6)).reshape((NX, NY, NZ, 6, F)).astype(jnp.int32),
    }


def from_lower(array, axis):
    count = array.shape[axis]
    kept = lax.slice_in_dim(array, 0, count - 1, axis=axis)
    zeros = jnp.zeros_like(lax.slice_in_dim(array, 0, 1, axis=axis))
    return jnp.concatenate([zeros, kept], axis=axis)

def from_upper(array, axis):
    count = array.shape[axis]
    kept = lax.slice_in_dim(array, 1, count, axis=axis)
    zeros = jnp.zeros_like(lax.slice_in_dim(array, 0, 1, axis=axis))
    return jnp.concatenate([kept, zeros], axis=axis)

def local_products(lowered, operator):
    shape = lowered.shape
    flat_rows = lowered.reshape((-1,) + shape[3:])
    flat_ops = operator.reshape((-1,) + operator.shape[3:])

    def single(pieces):
        return jnp.dot(pieces[0], pieces[1], preferred_element_type=jnp.float32).astype(jnp.bfloat16)
    return lax.map(single, (flat_rows, flat_ops)).reshape(shape)

def reference(seed_cotangent, trace_operator, face_matrices, saved_traces, edge_flags, node_map):
    width = face_matrices.shape[-1]
    span = 6 * width
    sweeps = saved_traces.shape[3]
    columns = seed_cotangent.shape[3]
    seeded = seed_cotangent.astype(jnp.float32)
    state = seeded
    total = jnp.zeros(face_matrices.shape, jnp.float32)
    for sweep in range(sweeps):
        hidden = local_products(state.astype(jnp.bfloat16), trace_operator)
        own = jnp.stack([hidden[..., number * width:(number + 1) * width] for number in range(6)], axis=3)
        received = jnp.stack([from_lower(own[:, :, :, 1], 0), from_upper(own[:, :, :, 0], 0), from_lower(own[:, :, :, 3], 1), from_upper(own[:, :, :, 2], 1), from_lower(own[:, :, :, 5], 2), from_upper(own[:, :, :, 4], 2)], axis=3)
        mapped = jnp.take_along_axis(received, node_map[:, :, :, :, None, :], axis=5)
        chosen = jnp.where(edge_flags[..., None, None] == 1, own, mapped)
        fresh = jnp.einsum('xyzkcf,xyzkfg->xyzkcg', chosen.astype(jnp.float32), face_matrices.astype(jnp.float32))
        state = jnp.concatenate([fresh[:, :, :, number] for number in range(6)] + [hidden[..., span:].astype(jnp.float32)], axis=-1) + seeded
        stored = saved_traces[:, :, :, sweeps - 1 - sweep]
        stored_faces = jnp.stack([stored[..., number * width:(number + 1) * width] for number in range(6)], axis=3)
        total = total + jnp.einsum('xyzkcf,xyzkcg->xyzkfg', chosen.astype(jnp.float32), stored_faces.astype(jnp.float32))
    adjoint_traces = state.astype(jnp.bfloat16)
    face_gradient = (total * (1.0 / jnp.sqrt(jnp.float32(columns)))).astype(jnp.bfloat16)
    return (adjoint_traces, face_gradient)
```

```python
import functools
import math

import jax
import jax.numpy as jnp
from jax import lax
from jax.experimental import pallas as pl
from jax.experimental.pallas import tpu as pltpu
from jax.sharding import PartitionSpec as P

LANES = 128
BLOCK = 256
AXES = ("gx", "gy", "gz")
BF16, F32 = jnp.bfloat16, jnp.float32
PAIRS = ((0, 1), (2, 3), (4, 5))
X, Y, Z = PAIRS


def up(value, step):
    return -(-value // step) * step


def dot(left, right):
    return jnp.dot(left, right, preferred_element_type=F32)


def span_of(width, face):
    base = face * width // LANES * LANES
    shift = face * width - base
    return base, shift, up(shift + width, LANES)


def widest(width):
    return max(span_of(width, face)[2] for face in range(6))


def take_face(value, shift, pad):
    if shift:
        value = pltpu.roll(value, value.shape[1] - shift, 1)
    return value[:, :pad].astype(BF16)


def segments(width, start, stop):
    edges = {start, stop}
    for face in range(6):
        base, _, extent = span_of(width, face)
        edges.update(edge for edge in (base, base + extent) if start < edge < stop)
    edges = sorted(edges)
    for low, high in zip(edges[:-1], edges[1:]):
        faces = []
        for face in range(6):
            base, _, extent = span_of(width, face)
            if base <= low and high <= base + extent:
                faces.append(face)
        yield low, high, faces


def add_faces(width, value, fresh, low, high, faces):
    for face in faces:
        base = span_of(width, face)[0]
        value = value + fresh[face][:, low - base : high - base]
    return value


def outer(mapped, stored):
    return lax.dot_general(
        mapped, stored, (((0,), (0,)), ((), ())), preferred_element_type=F32
    )


def exchange(
    width, seed_hbm, op_hbm, m_hbm, saved_hbm, map_hbm, flag_hbm,
    base_ref, inp_ref, sel_v, w_v, last_ref, g_v,
    seed_v, op_v, m_v, saved_v, map_v, flag_v, send_v, recv_v, old_v, mapped_v, packed_v,
    hid_v, stb_v, wide_v, in_sem, send_sem, recv_sem,
):
    columns, trace = seed_v.shape
    sweeps = saved_v.shape[0]
    pad = up(width, LANES)
    span = 6 * width
    x_end = up(2 * width, BLOCK)
    z_start = (4 * width) // BLOCK * BLOCK
    z_only = up(4 * width, BLOCK)
    tail = trace - LANES
    chunks = ((z_start, trace), (0, x_end), (x_end, z_start))

    where = [lax.axis_index(name) for name in AXES]
    has = []
    for axis, name in enumerate(AXES):
        has.append(where[axis] > 0)
        has.append(where[axis] < lax.axis_size(name) - 1)

    def peer(face):
        return {AXES[face // 2]: where[face // 2] + (1 if face % 2 else -1)}

    seed_in = pltpu.make_async_copy(seed_hbm, seed_v, in_sem.at[0])
    seed_in.start()
    op_in = []
    for number, (start, stop) in enumerate(chunks):
        copy = pltpu.make_async_copy(
            op_hbm.at[:, start:stop], op_v.at[:, start:stop], in_sem.at[1 + number]
        )
        copy.start()
        op_in.append(copy)
    flag_in = pltpu.make_async_copy(flag_hbm, flag_v, in_sem.at[7])
    flag_in.start()
    map_in = pltpu.make_async_copy(map_hbm, map_v, in_sem.at[6])
    map_in.start()
    m_in = pltpu.make_async_copy(m_hbm, m_v, in_sem.at[4])
    m_in.start()
    saved_in = pltpu.make_async_copy(saved_hbm, saved_v, in_sem.at[5])
    saved_in.start()

    barrier = pltpu.get_barrier_semaphore()
    count = 0
    for face in range(6):
        @pl.when(has[face])
        def _(face=face):
            pl.semaphore_signal(
                barrier, inc=1, device_id=peer(face), device_id_type=pl.DeviceIdType.MESH
            )
        count = count + has[face].astype(jnp.int32)

    for face in range(6):
        @pl.when(jnp.logical_not(has[face]))
        def _(face=face):
            for sweep in range(sweeps):
                recv_v[sweep, face] = jnp.zeros((columns, pad), BF16)

    def remote(sweep, face):
        return pltpu.make_async_remote_copy(
            src_ref=send_v.at[sweep, face],
            dst_ref=recv_v.at[sweep, face ^ 1],
            send_sem=send_sem.at[sweep, face],
            recv_sem=recv_sem.at[sweep, face ^ 1],
            device_id=peer(face),
            device_id_type=pl.DeviceIdType.MESH,
        )

    def arrival(sweep, face):
        return pltpu.make_async_remote_copy(
            src_ref=send_v.at[sweep, face],
            dst_ref=recv_v.at[sweep, face],
            send_sem=send_sem.at[sweep, face],
            recv_sem=recv_sem.at[sweep, face],
            device_id=peer(face),
            device_id_type=pl.DeviceIdType.MESH,
        )

    def emit(sweep, faces, value, start):
        for face in faces:
            base, shift, extent = span_of(width, face)
            send_v[sweep, face] = take_face(
                value[:, base - start : base - start + extent], shift, pad
            )
        for face in faces:
            @pl.when(has[face])
            def _(face=face):
                remote(sweep, face).start()

    def wait_for(sweep, faces):
        for face in faces:
            @pl.when(has[face])
            def _(face=face):
                arrival(sweep, face).wait_recv()

    def take(sweep, faces):
        found = {}
        for face in faces:
            inputs = lax.select(flag_v[face] == 1, send_v[sweep, face], recv_v[sweep, face])
            if sweep == sweeps - 1:
                inp_ref[face] = inputs
            else:
                old_v[sweep, face] = inputs
                extent = span_of(width, face)[2]
                found[face] = dot(inputs, w_v[face, :, 0:extent])
        return found

    def settle(fresh, start, stop):
        for low, high, faces in segments(width, start, stop):
            value = seed_v[:, low:high].astype(F32)
            value = add_faces(width, value, fresh, low, high, faces)
            if high > tail:
                cut = max(low, tail)
                place = lax.broadcasted_iota(jnp.int32, (columns, high - cut), 1) + cut
                inner = hid_v[:, cut:high].astype(BF16).astype(F32)
                inner = jnp.where(place >= span, inner, 0.0)
                end = value[:, cut - low :] + inner
                value = end if cut == low else jnp.concatenate([value[:, : cut - low], end], axis=1)
            stb_v[:, low:high] = value.astype(BF16)

    def map_inputs(sweep):
        for face in range(6):
            mapped_v[face, sweep * columns : (sweep + 1) * columns, :] = dot(
                old_v[sweep, face], sel_v[face]
            ).astype(BF16)

    def build_maps():
        flag_in.wait()
        map_in.wait()
        rows = lax.broadcasted_iota(jnp.int32, (pad, width), 0).astype(jnp.int16)
        lane = lax.broadcasted_iota(jnp.int32, (1, width), 1)
        for face in range(6):
            flag = (flag_v[face] == 1).astype(jnp.int32)
            row = map_v[face]
            row = row + (lane - row) * flag
            sel_v[face, :, width:pad] = jnp.zeros((pad, pad - width), BF16)
            sel_v[face, :, 0:width] = jnp.where(
                rows == row.astype(jnp.int16), jnp.bfloat16(1.0), jnp.bfloat16(0.0)
            )
        m_in.wait()
        for slot in range(2):
            wide_v[slot, :, pad - LANES :] = jnp.zeros(
                (pad, wide_v.shape[2] - pad + LANES), F32
            )
        for face in range(6):
            _, shift, extent = span_of(width, face)
            wide_v[face % 2, :, 0:width] = dot(sel_v[face, :, 0:width], m_v[face])
            value = wide_v[face % 2, :, 0:extent]
            if shift:
                value = pltpu.roll(value, shift, 1)
            w_v[face, :, 0:extent] = value.astype(BF16)

    def pack():
        saved_in.wait()
        for face in range(6):
            base, shift, extent = span_of(width, face)
            for step in range(sweeps):
                value = take_face(
                    saved_v[sweeps - 1 - step, :, base : base + extent].astype(F32), shift, pad
                )
                if step == sweeps - 1:
                    last_ref[face] = value
                else:
                    packed_v[face, step * columns : (step + 1) * columns, :] = value

    y_low = span_of(width, 2)[0]
    y_high = span_of(width, 3)[0] + span_of(width, 3)[2]

    def send_all(sweep, hidden_of):
        value = hidden_of(0)
        if sweep == 0:
            pl.semaphore_wait(barrier, count)
        emit(sweep, Z, value, z_start)
        hid_v[:, z_start:y_high] = value[:, : y_high - z_start]
        hid_v[:, tail:trace] = value[:, tail - z_start :]
        value = hidden_of(1)
        emit(sweep, X, value, 0)
        hid_v[:, y_low:x_end] = value[:, y_low:]
        value = hidden_of(2)
        value = jnp.concatenate([hid_v[:, y_low:x_end], value, hid_v[:, z_start:y_high]], axis=1)
        emit(sweep, Y, value, y_low)

    seed_in.wait()

    def first(number):
        start, stop = chunks[number]
        op_in[number].wait()
        return dot(seed_v[...], op_v[:, start:stop])

    send_all(0, first)
    build_maps()
    for sweep in range(sweeps - 1):
        wait_for(sweep, Z)
        fresh = take(sweep, Z)
        settle(fresh, z_only, trace)
        ahead = dot(stb_v[:, z_only:trace], op_v[z_only:trace, z_start:trace])
        wait_for(sweep, X)
        wait_for(sweep, Y)
        fresh.update(take(sweep, X))
        fresh.update(take(sweep, Y))
        settle(fresh, 0, z_only)

        def later(number, ahead=ahead):
            start, stop = chunks[number]
            if number == 0:
                return ahead + dot(stb_v[:, 0:z_only], op_v[0:z_only, start:stop])
            return dot(stb_v[...], op_v[:, start:stop])

        send_all(sweep + 1, later)
        if sweep == 0:
            pack()
        map_inputs(sweep)

    for face in range(6):
        g_v[face] = outer(mapped_v[face], packed_v[face])
    base_ref[...] = seed_v[...].astype(F32)
    inner = hid_v[:, tail:trace].astype(BF16).astype(F32)
    place = lax.broadcasted_iota(jnp.int32, (columns, LANES), 1) + tail
    base_ref[:, tail:trace] += jnp.where(place >= span, inner, 0.0)
    for faces in (Z, X, Y):
        wait_for(sweeps - 1, faces)
        take(sweeps - 1, faces)
    for sweep in range(sweeps):
        for face in range(6):
            @pl.when(has[face])
            def _(face=face, sweep=sweep):
                remote(sweep, face).wait_send()


def finish(
    width, base_ref, inp_ref, sel_ref, w_ref, last_ref, g_ref, adjoint_hbm, gradient_hbm,
    adjoint_v, gradient_v, out_sem,
):
    columns, trace = base_ref.shape
    scale = 1.0 / math.sqrt(columns)
    fresh = {}
    for face in range(6):
        fresh[face] = dot(inp_ref[face], w_ref[face, :, 0 : span_of(width, face)[2]])
    for low, high, faces in segments(width, 0, trace):
        value = add_faces(width, base_ref[:, low:high], fresh, low, high, faces)
        adjoint_v[:, low:high] = value.astype(BF16)
    copies = [pltpu.make_async_copy(adjoint_v, adjoint_hbm, out_sem.at[6])]
    copies[0].start()
    for face in range(6):
        mapped = dot(inp_ref[face], sel_ref[face]).astype(BF16)
        total = g_ref[face] + outer(mapped, last_ref[face])
        gradient_v[face] = (total * scale).astype(BF16)[0:width, 0:width]
        copy = pltpu.make_async_copy(gradient_v.at[face], gradient_hbm.at[face], out_sem.at[face])
        copy.start()
        copies.append(copy)
    for copy in copies:
        copy.wait()


def local(seed_cotangent, trace_operator, face_matrices, saved_traces, edge_flags, node_map):
    seed, operator, matrices, stored, flags, mapping = (
        array.reshape(array.shape[3:])
        for array in (
            seed_cotangent, trace_operator, face_matrices, saved_traces, edge_flags, node_map
        )
    )
    width = matrices.shape[-1]
    sweeps, columns, trace = stored.shape
    pad = up(width, LANES)
    wide = widest(width)
    anywhere = pl.BlockSpec(memory_space=pltpu.HBM)
    resident = pl.BlockSpec(memory_space=pltpu.VMEM)
    between = pl.pallas_call(
        functools.partial(exchange, width),
        out_shape=(
            jax.ShapeDtypeStruct(seed.shape, F32),
            jax.ShapeDtypeStruct((6, columns, pad), BF16),
            jax.ShapeDtypeStruct((6, pad, pad), BF16),
            jax.ShapeDtypeStruct((6, pad, wide), BF16),
            jax.ShapeDtypeStruct((6, columns, pad), BF16),
            jax.ShapeDtypeStruct((6, pad, pad), F32),
        ),
        in_specs=[anywhere] * 6,
        out_specs=(resident,) * 6,
        scratch_shapes=[
            pltpu.VMEM(seed.shape, BF16),
            pltpu.VMEM(operator.shape, BF16),
            pltpu.VMEM(matrices.shape, BF16),
            pltpu.VMEM(stored.shape, BF16),
            pltpu.VMEM((6, 1, width), jnp.int32),
            pltpu.SMEM(flags.shape, jnp.int32),
            pltpu.VMEM((sweeps, 6, columns, pad), BF16),
            pltpu.VMEM((sweeps, 6, columns, pad), BF16),
            pltpu.VMEM((sweeps - 1, 6, columns, pad), BF16),
            pltpu.VMEM((6, (sweeps - 1) * columns, pad), BF16),
            pltpu.VMEM((6, (sweeps - 1) * columns, pad), BF16),
            pltpu.VMEM(seed.shape, F32),
            pltpu.VMEM(seed.shape, BF16),
            pltpu.VMEM((2, pad, wide), F32),
            pltpu.SemaphoreType.DMA((8,)),
            pltpu.SemaphoreType.DMA((sweeps, 6)),
            pltpu.SemaphoreType.DMA((sweeps, 6)),
        ],
        compiler_params=pltpu.CompilerParams(
            collective_id=0, has_side_effects=True, vmem_limit_bytes=40 * 1024 * 1024
        ),
    )(*(pltpu.with_memory_space_constraint(array, pltpu.HBM) for array in (seed, operator, matrices, stored, mapping[:, None, :], flags)))
    adjoint, gradient = pl.pallas_call(
        functools.partial(finish, width),
        out_shape=(
            jax.ShapeDtypeStruct(seed.shape, BF16),
            jax.ShapeDtypeStruct(matrices.shape, BF16),
        ),
        in_specs=[resident] * 6,
        out_specs=(anywhere, anywhere),
        scratch_shapes=[
            pltpu.VMEM(seed.shape, BF16),
            pltpu.VMEM(matrices.shape, BF16),
            pltpu.SemaphoreType.DMA((7,)),
        ],
        compiler_params=pltpu.CompilerParams(vmem_limit_bytes=12 * 1024 * 1024),
    )(*between)
    return adjoint[None, None, None], gradient[None, None, None]


def solution(mesh):
    return jax.shard_map(
        local,
        mesh=mesh,
        in_specs=(
            P("gx", "gy", "gz", None, None),
            P("gx", "gy", "gz", None, None),
            P("gx", "gy", "gz", None, None, None),
            P("gx", "gy", "gz", None, None, None),
            P("gx", "gy", "gz", None),
            P("gx", "gy", "gz", None, None),
        ),
        out_specs=(P("gx", "gy", "gz", None, None), P("gx", "gy", "gz", None, None, None)),
        check_vma=False,
    )
```

```python
import functools
import math

import jax
import jax.numpy as jnp
from jax import lax
from jax.experimental import pallas as pl
from jax.experimental.pallas import tpu as pltpu
from jax.sharding import PartitionSpec as P

LANES = 128
BLOCK = 256
AHEAD = 2
AXES = ("gx", "gy", "gz")
BF16, F32 = jnp.bfloat16, jnp.float32
PAIRS = ((0, 1), (2, 3), (4, 5))
X, Y, Z = PAIRS


def up(value, step):
    return -(-value // step) * step


def dot(left, right):
    return jnp.dot(left, right, preferred_element_type=F32)


def span_of(width, face):
    base = face * width // LANES * LANES
    shift = face * width - base
    return base, shift, up(shift + width, LANES)


def groups_of(width, trace):
    tiles = trace // BLOCK
    z_tile = 4 * width // BLOCK
    x_tile = up(2 * width, BLOCK) // BLOCK
    order = list(range(tiles - 1, z_tile - 1, -1))
    order += list(range(x_tile)) + list(range(x_tile, z_tile))
    groups, done, sent = [], set(), set()
    for first in range(0, tiles, 2):
        group = sorted(order[first : first + 2])
        done.update(group)
        faces = []
        for face in (5, 4, 0, 1, 2, 3):
            base, _, extent = span_of(width, face)
            needs = range(base // BLOCK, up(base + extent, BLOCK) // BLOCK)
            if face not in sent and done.issuperset(needs):
                faces.append(face)
        sent.update(faces)
        groups.append((group, faces))
    return groups


def runs_of(group):
    runs = []
    for tile in group:
        if runs and runs[-1][1] == tile * BLOCK:
            runs[-1] = (runs[-1][0], (tile + 1) * BLOCK)
        else:
            runs.append((tile * BLOCK, (tile + 1) * BLOCK))
    return runs


def gather(ref, low, high, runs):
    parts = [ref[low:high, start:stop] for start, stop in runs]
    return parts[0] if len(parts) == 1 else jnp.concatenate(parts, axis=1)


def widest(width):
    return max(span_of(width, face)[2] for face in range(6))


def take_face(value, shift, pad):
    if shift:
        value = pltpu.roll(value, value.shape[1] - shift, 1)
    return value[:, :pad].astype(BF16)


def segments(width, start, stop):
    edges = {start, stop}
    for face in range(6):
        base, _, extent = span_of(width, face)
        edges.update(edge for edge in (base, base + extent) if start < edge < stop)
    edges = sorted(edges)
    for low, high in zip(edges[:-1], edges[1:]):
        faces = []
        for face in range(6):
            base, _, extent = span_of(width, face)
            if base <= low and high <= base + extent:
                faces.append(face)
        yield low, high, faces


def add_faces(width, value, fresh, low, high, faces):
    for face in faces:
        base = span_of(width, face)[0]
        value = value + fresh[face][:, low - base : high - base]
    return value


def outer(mapped, stored):
    return lax.dot_general(
        mapped, stored, (((0,), (0,)), ((), ())), preferred_element_type=F32
    )


def scaled(width, mapped, total, stored, columns):
    total = total + outer(mapped, stored)
    return (total * (1.0 / math.sqrt(columns))).astype(BF16)[0:width, 0:width]


def exchange(
    width, seed_hbm, op_hbm, m_hbm, saved_hbm, map_hbm, flag_hbm,
    base_ref, inp_ref, given_ref, sel_v, w_v, last_ref, g_v,
    seed_v, op_v, m_v, saved_v, map_v, flag_v, send_v, recv_v, old_v, mapped_v, packed_v,
    hid_v, stb_v, wide_v, in_sem, op_sem, send_sem, recv_sem,
):
    columns, trace = seed_v.shape
    sweeps = saved_v.shape[0]
    pad = up(width, LANES)
    span = 6 * width
    x_only = 2 * width // BLOCK * BLOCK
    z_only = up(4 * width, BLOCK)
    tail = trace - LANES
    groups = groups_of(width, trace)
    runs = [runs_of(group) for group, _ in groups]

    where = [lax.axis_index(name) for name in AXES]
    has = []
    for axis, name in enumerate(AXES):
        has.append(where[axis] > 0)
        has.append(where[axis] < lax.axis_size(name) - 1)

    def peer(face):
        return {AXES[face // 2]: where[face // 2] + (1 if face % 2 else -1)}

    seed_in = pltpu.make_async_copy(seed_hbm, seed_v, in_sem.at[0])
    seed_in.start()
    op_in = []
    for number, group in enumerate(runs):
        copies = []
        for part, (start, stop) in enumerate(group):
            copy = pltpu.make_async_copy(
                op_hbm.at[:, start:stop], op_v.at[:, start:stop], op_sem.at[number, part]
            )
            copy.start()
            copies.append(copy)
        op_in.append(copies)
    flag_in = pltpu.make_async_copy(flag_hbm, flag_v, in_sem.at[1])
    flag_in.start()
    map_in = pltpu.make_async_copy(map_hbm, map_v, in_sem.at[2])
    map_in.start()
    m_in = pltpu.make_async_copy(m_hbm, m_v, in_sem.at[3])
    saved_in = pltpu.make_async_copy(saved_hbm, saved_v, in_sem.at[4])

    barrier = pltpu.get_barrier_semaphore()
    count = 0
    for face in range(6):
        @pl.when(has[face])
        def _(face=face):
            pl.semaphore_signal(
                barrier, inc=1, device_id=peer(face), device_id_type=pl.DeviceIdType.MESH
            )
        count = count + has[face].astype(jnp.int32)

    for face in range(6):
        @pl.when(jnp.logical_not(has[face]))
        def _(face=face):
            for sweep in range(sweeps):
                recv_v[sweep, face] = jnp.zeros((columns, pad), BF16)

    def remote(sweep, face):
        return pltpu.make_async_remote_copy(
            src_ref=send_v.at[sweep, face],
            dst_ref=recv_v.at[sweep, face ^ 1],
            send_sem=send_sem.at[sweep, face],
            recv_sem=recv_sem.at[sweep, face ^ 1],
            device_id=peer(face),
            device_id_type=pl.DeviceIdType.MESH,
        )

    def arrival(sweep, face):
        return pltpu.make_async_remote_copy(
            src_ref=send_v.at[sweep, face],
            dst_ref=recv_v.at[sweep, face],
            send_sem=send_sem.at[sweep, face],
            recv_sem=recv_sem.at[sweep, face],
            device_id=peer(face),
            device_id_type=pl.DeviceIdType.MESH,
        )

    def fill(sweep, faces):
        for face in faces:
            base, shift, extent = span_of(width, face)
            send_v[sweep, face] = take_face(hid_v[:, base : base + extent], shift, pad)

    def launch(sweep, faces):
        for face in faces:
            @pl.when(has[face])
            def _(face=face):
                remote(sweep, face).start()

    def put(number, value, more):
        at = 0
        for start, stop in runs[number]:
            piece = value[:, at : at + stop - start]
            hid_v[:, start:stop] = hid_v[:, start:stop] + piece if more else piece
            at += stop - start

    def wait_for(sweep, faces):
        for face in faces:
            @pl.when(has[face])
            def _(face=face):
                arrival(sweep, face).wait_recv()

    def take(sweep, faces):
        found = {}
        for face in faces:
            inputs = lax.select(flag_v[face] == 1, send_v[sweep, face], recv_v[sweep, face])
            if sweep == sweeps - 1:
                inp_ref[face] = inputs
            else:
                old_v[sweep, face] = inputs
                extent = span_of(width, face)[2]
                found[face] = dot(inputs, w_v[face, :, 0:extent])
        return found

    def settle(fresh, start, stop):
        for low, high, faces in segments(width, start, stop):
            value = seed_v[:, low:high].astype(F32)
            value = add_faces(width, value, fresh, low, high, faces)
            if high > tail:
                cut = max(low, tail)
                place = lax.broadcasted_iota(jnp.int32, (columns, high - cut), 1) + cut
                inner = hid_v[:, cut:high].astype(BF16).astype(F32)
                inner = jnp.where(place >= span, inner, 0.0)
                end = value[:, cut - low :] + inner
                value = end if cut == low else jnp.concatenate([value[:, : cut - low], end], axis=1)
            stb_v[:, low:high] = value.astype(BF16)

    def map_inputs(sweep):
        for face in range(6):
            mapped_v[face, sweep * columns : (sweep + 1) * columns, :] = dot(
                old_v[sweep, face], sel_v[face]
            ).astype(BF16)

    def build_maps():
        flag_in.wait()
        map_in.wait()
        rows = lax.broadcasted_iota(jnp.int32, (pad, width), 0).astype(jnp.int16)
        lane = lax.broadcasted_iota(jnp.int32, (1, width), 1)
        for face in range(6):
            flag = (flag_v[face] == 1).astype(jnp.int32)
            row = map_v[face]
            row = row + (lane - row) * flag
            sel_v[face, :, width:pad] = jnp.zeros((pad, pad - width), BF16)
            sel_v[face, :, 0:width] = jnp.where(
                rows == row.astype(jnp.int16), jnp.bfloat16(1.0), jnp.bfloat16(0.0)
            )
        m_in.wait()
        for slot in range(2):
            wide_v[slot, :, pad - LANES :] = jnp.zeros(
                (pad, wide_v.shape[2] - pad + LANES), F32
            )
        for face in range(6):
            _, shift, extent = span_of(width, face)
            wide_v[face % 2, :, 0:width] = dot(sel_v[face, :, 0:width], m_v[face])
            value = wide_v[face % 2, :, 0:extent]
            if shift:
                value = pltpu.roll(value, shift, 1)
            w_v[face, :, 0:extent] = value.astype(BF16)

    def pack():
        saved_in.wait()
        for face in range(6):
            base, shift, extent = span_of(width, face)
            for step in range(sweeps):
                value = take_face(
                    saved_v[sweeps - 1 - step, :, base : base + extent].astype(F32), shift, pad
                )
                if step == sweeps - 1:
                    last_ref[face] = value
                else:
                    packed_v[face, step * columns : (step + 1) * columns, :] = value

    def multiply(number, low, high, more, left=stb_v):
        put(number, dot(left[:, low:high], gather(op_v, low, high, runs[number])), more)

    seed_in.wait()
    for number, (_, faces) in enumerate(groups):
        for copy in op_in[number]:
            copy.wait()
        multiply(number, 0, trace, False, seed_v)
        fill(0, faces)
        if number == 0:
            pl.semaphore_wait(barrier, count)
        launch(0, faces)
    m_in.start()
    saved_in.start()
    build_maps()
    half = up(trace // 2, BLOCK)
    for sweep in range(sweeps - 1):
        wait_for(sweep, Z)
        fresh = take(sweep, Z)
        settle(fresh, z_only, trace)
        wait_for(sweep, X)
        fresh.update(take(sweep, X))
        for number in range(AHEAD):
            multiply(number, z_only, trace, False)
        settle(fresh, 0, x_only)
        wait_for(sweep, Y)
        fresh.update(take(sweep, Y))
        multiply(0, 0, x_only, True)
        settle(fresh, x_only, z_only)
        multiply(0, x_only, z_only, True)
        for number, (_, faces) in enumerate(groups):
            following = number + 1
            ahead = following < AHEAD
            if following < len(groups):
                multiply(following, 0, half, ahead)
            fill(sweep + 1, faces)
            launch(sweep + 1, faces)
            if following < len(groups):
                multiply(following, half, z_only if ahead else trace, True)
        if sweep == 0:
            pack()
        map_inputs(sweep)

    for face in range(6):
        g_v[face] = outer(mapped_v[face], packed_v[face])
    base_ref[...] = seed_v[...].astype(F32)
    inner = hid_v[:, tail:trace].astype(BF16).astype(F32)
    place = lax.broadcasted_iota(jnp.int32, (columns, LANES), 1) + tail
    base_ref[:, tail:trace] += jnp.where(place >= span, inner, 0.0)
    for pair in (Z, X):
        wait_for(sweeps - 1, pair)
        take(sweeps - 1, pair)
        for face in pair:
            given_ref[face] = dot(inp_ref[face], sel_v[face]).astype(BF16)
    wait_for(sweeps - 1, Y)
    take(sweeps - 1, Y)
    for sweep in range(sweeps):
        for face in range(6):
            @pl.when(has[face])
            def _(face=face, sweep=sweep):
                remote(sweep, face).wait_send()


def finish(
    width, base_ref, inp_ref, given_ref, sel_ref, w_ref, last_ref, g_ref,
    adjoint_hbm, gradient_hbm, adjoint_v, gradient_v, mapped_v, out_sem,
):
    columns, trace = base_ref.shape
    copies = []

    def write(source, target):
        copy = pltpu.make_async_copy(source, target, out_sem.at[len(copies)])
        copy.start()
        copies.append(copy)

    def grade(faces, mapped):
        for face in faces:
            gradient_v[face] = scaled(width, mapped[face][...], g_ref[face], last_ref[face], columns)
        part = slice(faces[0], faces[-1] + 1)
        write(gradient_v.at[part], gradient_hbm.at[part])

    for face in Y:
        mapped_v[face - Y[0]] = dot(inp_ref[face], sel_ref[face]).astype(BF16)
    grade(Z, given_ref)
    grade(X, given_ref)
    fresh = {}
    for face in range(6):
        fresh[face] = dot(inp_ref[face], w_ref[face, :, 0 : span_of(width, face)[2]])
    for low, high, faces in segments(width, 0, trace):
        value = add_faces(width, base_ref[:, low:high], fresh, low, high, faces)
        adjoint_v[:, low:high] = value.astype(BF16)
    write(adjoint_v, adjoint_hbm)
    grade(Y, [None, None, mapped_v.at[0], mapped_v.at[1]])
    for copy in copies:
        copy.wait()


def local(seed_cotangent, trace_operator, face_matrices, saved_traces, edge_flags, node_map):
    seed, operator, matrices, stored, flags, mapping = (
        array.reshape(array.shape[3:])
        for array in (
            seed_cotangent, trace_operator, face_matrices, saved_traces, edge_flags, node_map
        )
    )
    width = matrices.shape[-1]
    sweeps, columns, trace = stored.shape
    pad = up(width, LANES)
    wide = widest(width)
    anywhere = pl.BlockSpec(memory_space=pltpu.HBM)
    resident = pl.BlockSpec(memory_space=pltpu.VMEM)
    between = pl.pallas_call(
        functools.partial(exchange, width),
        out_shape=(
            jax.ShapeDtypeStruct(seed.shape, F32),
            jax.ShapeDtypeStruct((6, columns, pad), BF16),
            jax.ShapeDtypeStruct((6, columns, pad), BF16),
            jax.ShapeDtypeStruct((6, pad, pad), BF16),
            jax.ShapeDtypeStruct((6, pad, wide), BF16),
            jax.ShapeDtypeStruct((6, columns, pad), BF16),
            jax.ShapeDtypeStruct((6, pad, pad), F32),
        ),
        in_specs=[anywhere] * 6,
        out_specs=(resident,) * 7,
        scratch_shapes=[
            pltpu.VMEM(seed.shape, BF16),
            pltpu.VMEM(operator.shape, BF16),
            pltpu.VMEM(matrices.shape, BF16),
            pltpu.VMEM(stored.shape, BF16),
            pltpu.VMEM((6, 1, width), jnp.int32),
            pltpu.SMEM(flags.shape, jnp.int32),
            pltpu.VMEM((sweeps, 6, columns, pad), BF16),
            pltpu.VMEM((sweeps, 6, columns, pad), BF16),
            pltpu.VMEM((sweeps - 1, 6, columns, pad), BF16),
            pltpu.VMEM((6, (sweeps - 1) * columns, pad), BF16),
            pltpu.VMEM((6, (sweeps - 1) * columns, pad), BF16),
            pltpu.VMEM(seed.shape, F32),
            pltpu.VMEM(seed.shape, BF16),
            pltpu.VMEM((2, pad, wide), F32),
            pltpu.SemaphoreType.DMA((5,)),
            pltpu.SemaphoreType.DMA((trace // BLOCK // 2, 2)),
            pltpu.SemaphoreType.DMA((sweeps, 6)),
            pltpu.SemaphoreType.DMA((sweeps, 6)),
        ],
        compiler_params=pltpu.CompilerParams(
            collective_id=0, has_side_effects=True, vmem_limit_bytes=40 * 1024 * 1024
        ),
    )(*(pltpu.with_memory_space_constraint(array, pltpu.HBM) for array in (seed, operator, matrices, stored, mapping[:, None, :], flags)))
    adjoint, gradient = pl.pallas_call(
        functools.partial(finish, width),
        out_shape=(
            jax.ShapeDtypeStruct(seed.shape, BF16),
            jax.ShapeDtypeStruct(matrices.shape, BF16),
        ),
        in_specs=[resident] * 7,
        out_specs=(anywhere, anywhere),
        scratch_shapes=[
            pltpu.VMEM(seed.shape, BF16),
            pltpu.VMEM(matrices.shape, BF16),
            pltpu.VMEM((2, columns, pad), BF16),
            pltpu.SemaphoreType.DMA((4,)),
        ],
        compiler_params=pltpu.CompilerParams(vmem_limit_bytes=12 * 1024 * 1024),
    )(*between)
    return adjoint[None, None, None], gradient[None, None, None]


def solution(mesh):
    return jax.shard_map(
        local,
        mesh=mesh,
        in_specs=(
            P("gx", "gy", "gz", None, None),
            P("gx", "gy", "gz", None, None),
            P("gx", "gy", "gz", None, None, None),
            P("gx", "gy", "gz", None, None, None),
            P("gx", "gy", "gz", None),
            P("gx", "gy", "gz", None, None),
        ),
        out_specs=(P("gx", "gy", "gz", None, None), P("gx", "gy", "gz", None, None, None)),
        check_vma=False,
    )
```

```python
import functools
import math

import jax
import jax.numpy as jnp
from jax import lax
from jax.experimental import pallas as pl
from jax.experimental.pallas import tpu as pltpu
from jax.sharding import PartitionSpec as P

LANES = 128
BLOCK = 256
AHEAD = 2
AXES = ("gx", "gy", "gz")
BF16, F32 = jnp.bfloat16, jnp.float32
PAIRS = ((0, 1), (2, 3), (4, 5))
X, Y, Z = PAIRS


def up(value, step):
    return -(-value // step) * step


def dot(left, right):
    return jnp.dot(left, right, preferred_element_type=F32)


def span_of(width, face):
    base = face * width // LANES * LANES
    shift = face * width - base
    return base, shift, up(shift + width, LANES)


def groups_of(width, trace):
    tiles = trace // BLOCK
    order = list(range(4 * width // BLOCK, up(5 * width, BLOCK) // BLOCK))
    order += [tile for tile in range(tiles) if tile not in order]
    groups, done, sent = [], set(), set()
    for first in range(0, tiles, 2):
        group = sorted(order[first : first + 2])
        done.update(group)
        faces = []
        for face in (4, 0, 2, 1, 5, 3):
            base, _, extent = span_of(width, face)
            needs = range(base // BLOCK, up(base + extent, BLOCK) // BLOCK)
            if face not in sent and done.issuperset(needs):
                faces.append(face)
        sent.update(faces)
        groups.append((group, faces))
    return groups


def runs_of(group):
    runs = []
    for tile in group:
        if runs and runs[-1][1] == tile * BLOCK:
            runs[-1] = (runs[-1][0], (tile + 1) * BLOCK)
        else:
            runs.append((tile * BLOCK, (tile + 1) * BLOCK))
    return runs


def gather(ref, low, high, runs):
    parts = [ref[low:high, start:stop] for start, stop in runs]
    return parts[0] if len(parts) == 1 else jnp.concatenate(parts, axis=1)


def widest(width):
    return max(span_of(width, face)[2] for face in range(6))


def take_face(value, shift, pad):
    if shift:
        value = pltpu.roll(value, value.shape[1] - shift, 1)
    return value[:, :pad].astype(BF16)


def segments(width, start, stop):
    edges = {start, stop}
    for face in range(6):
        base, _, extent = span_of(width, face)
        edges.update(edge for edge in (base, base + extent) if start < edge < stop)
    edges = sorted(edges)
    for low, high in zip(edges[:-1], edges[1:]):
        faces = []
        for face in range(6):
            base, _, extent = span_of(width, face)
            if base <= low and high <= base + extent:
                faces.append(face)
        yield low, high, faces


def add_faces(width, value, fresh, low, high, faces):
    for face in faces:
        base = span_of(width, face)[0]
        value = value + fresh[face][:, low - base : high - base]
    return value


def outer(mapped, stored):
    return lax.dot_general(
        mapped, stored, (((0,), (0,)), ((), ())), preferred_element_type=F32
    )


def scaled(width, mapped, total, stored, columns):
    total = total + outer(mapped, stored)
    return (total * (1.0 / math.sqrt(columns))).astype(BF16)[0:width, 0:width]


def exchange(
    width, seed_hbm, op_hbm, m_hbm, saved_hbm, map_hbm, flag_hbm,
    base_ref, inp_ref, given_ref, sel_v, w_v, last_ref, g_v,
    seed_v, op_v, m_v, saved_v, map_v, flag_v, send_v, recv_v, old_v, mapped_v, packed_v,
    hid_v, stb_v, wide_v, in_sem, op_sem, send_sem, recv_sem,
):
    columns, trace = seed_v.shape
    sweeps = saved_v.shape[0]
    pad = up(width, LANES)
    span = 6 * width
    x_only = 2 * width // BLOCK * BLOCK
    z_only = up(4 * width, BLOCK)
    tail = trace - LANES
    groups = groups_of(width, trace)
    runs = [runs_of(group) for group, _ in groups]

    where = [lax.axis_index(name) for name in AXES]
    has = []
    for axis, name in enumerate(AXES):
        has.append(where[axis] > 0)
        has.append(where[axis] < lax.axis_size(name) - 1)

    def peer(face):
        return {AXES[face // 2]: where[face // 2] + (1 if face % 2 else -1)}

    seed_in = pltpu.make_async_copy(seed_hbm, seed_v, in_sem.at[0])
    seed_in.start()
    op_in = []
    for number, group in enumerate(runs):
        copies = []
        for part, (start, stop) in enumerate(group):
            copy = pltpu.make_async_copy(
                op_hbm.at[:, start:stop], op_v.at[:, start:stop], op_sem.at[number, part]
            )
            copy.start()
            copies.append(copy)
        op_in.append(copies)
    flag_in = pltpu.make_async_copy(flag_hbm, flag_v, in_sem.at[1])
    flag_in.start()
    map_in = pltpu.make_async_copy(map_hbm, map_v, in_sem.at[2])
    map_in.start()
    m_in = pltpu.make_async_copy(m_hbm, m_v, in_sem.at[3])
    saved_in = pltpu.make_async_copy(saved_hbm, saved_v, in_sem.at[4])

    barrier = pltpu.get_barrier_semaphore()
    count = 0
    for face in range(6):
        @pl.when(has[face])
        def _(face=face):
            pl.semaphore_signal(
                barrier, inc=1, device_id=peer(face), device_id_type=pl.DeviceIdType.MESH
            )
        count = count + has[face].astype(jnp.int32)

    for face in range(6):
        @pl.when(jnp.logical_not(has[face]))
        def _(face=face):
            for sweep in range(sweeps):
                recv_v[sweep, face] = jnp.zeros((columns, pad), BF16)

    def remote(sweep, face):
        return pltpu.make_async_remote_copy(
            src_ref=send_v.at[sweep, face],
            dst_ref=recv_v.at[sweep, face ^ 1],
            send_sem=send_sem.at[sweep, face],
            recv_sem=recv_sem.at[sweep, face ^ 1],
            device_id=peer(face),
            device_id_type=pl.DeviceIdType.MESH,
        )

    def arrival(sweep, face):
        return pltpu.make_async_remote_copy(
            src_ref=send_v.at[sweep, face],
            dst_ref=recv_v.at[sweep, face],
            send_sem=send_sem.at[sweep, face],
            recv_sem=recv_sem.at[sweep, face],
            device_id=peer(face),
            device_id_type=pl.DeviceIdType.MESH,
        )

    def fill(sweep, faces):
        for face in faces:
            base, shift, extent = span_of(width, face)
            send_v[sweep, face] = take_face(hid_v[:, base : base + extent], shift, pad)

    def launch(sweep, faces):
        for face in faces:
            @pl.when(has[face])
            def _(face=face):
                remote(sweep, face).start()

    def put(number, value, more):
        at = 0
        for start, stop in runs[number]:
            piece = value[:, at : at + stop - start]
            hid_v[:, start:stop] = hid_v[:, start:stop] + piece if more else piece
            at += stop - start

    def wait_for(sweep, faces):
        for face in faces:
            @pl.when(has[face])
            def _(face=face):
                arrival(sweep, face).wait_recv()

    def take(sweep, faces):
        found = {}
        for face in faces:
            inputs = lax.select(flag_v[face] == 1, send_v[sweep, face], recv_v[sweep, face])
            if sweep == sweeps - 1:
                inp_ref[face] = inputs
            else:
                old_v[sweep, face] = inputs
                extent = span_of(width, face)[2]
                found[face] = dot(inputs, w_v[face, :, 0:extent])
        return found

    def settle(fresh, start, stop):
        for low, high, faces in segments(width, start, stop):
            value = seed_v[:, low:high].astype(F32)
            value = add_faces(width, value, fresh, low, high, faces)
            if high > tail:
                cut = max(low, tail)
                place = lax.broadcasted_iota(jnp.int32, (columns, high - cut), 1) + cut
                inner = hid_v[:, cut:high].astype(BF16).astype(F32)
                inner = jnp.where(place >= span, inner, 0.0)
                end = value[:, cut - low :] + inner
                value = end if cut == low else jnp.concatenate([value[:, : cut - low], end], axis=1)
            stb_v[:, low:high] = value.astype(BF16)

    def map_inputs(sweep):
        for face in range(6):
            mapped_v[face, sweep * columns : (sweep + 1) * columns, :] = dot(
                old_v[sweep, face], sel_v[face]
            ).astype(BF16)

    def build_maps():
        flag_in.wait()
        map_in.wait()
        rows = lax.broadcasted_iota(jnp.int32, (pad, width), 0).astype(jnp.int16)
        lane = lax.broadcasted_iota(jnp.int32, (1, width), 1)
        for face in range(6):
            flag = (flag_v[face] == 1).astype(jnp.int32)
            row = map_v[face]
            row = row + (lane - row) * flag
            sel_v[face, :, width:pad] = jnp.zeros((pad, pad - width), BF16)
            sel_v[face, :, 0:width] = jnp.where(
                rows == row.astype(jnp.int16), jnp.bfloat16(1.0), jnp.bfloat16(0.0)
            )
        m_in.wait()
        for slot in range(2):
            wide_v[slot, :, pad - LANES :] = jnp.zeros(
                (pad, wide_v.shape[2] - pad + LANES), F32
            )
        for face in range(6):
            _, shift, extent = span_of(width, face)
            wide_v[face % 2, :, 0:width] = dot(sel_v[face, :, 0:width], m_v[face])
            value = wide_v[face % 2, :, 0:extent]
            if shift:
                value = pltpu.roll(value, shift, 1)
            w_v[face, :, 0:extent] = value.astype(BF16)

    def pack():
        saved_in.wait()
        for face in range(6):
            base, shift, extent = span_of(width, face)
            for step in range(sweeps):
                value = take_face(
                    saved_v[sweeps - 1 - step, :, base : base + extent].astype(F32), shift, pad
                )
                if step == sweeps - 1:
                    last_ref[face] = value
                else:
                    packed_v[face, step * columns : (step + 1) * columns, :] = value

    def multiply(number, low, high, more, left=stb_v):
        put(number, dot(left[:, low:high], gather(op_v, low, high, runs[number])), more)

    seed_in.wait()
    for number, (_, faces) in enumerate(groups):
        for copy in op_in[number]:
            copy.wait()
        multiply(number, 0, trace, False, seed_v)
        fill(0, faces)
        if number == 0:
            pl.semaphore_wait(barrier, count)
        launch(0, faces)
    m_in.start()
    saved_in.start()
    build_maps()
    half = up(trace // 2, BLOCK)
    for sweep in range(sweeps - 1):
        wait_for(sweep, Z)
        fresh = take(sweep, Z)
        settle(fresh, z_only, trace)
        wait_for(sweep, X)
        fresh.update(take(sweep, X))
        for number in range(AHEAD):
            multiply(number, z_only, trace, False)
        settle(fresh, 0, x_only)
        wait_for(sweep, Y)
        fresh.update(take(sweep, Y))
        multiply(0, 0, x_only, True)
        settle(fresh, x_only, z_only)
        multiply(0, x_only, z_only, True)
        for number, (_, faces) in enumerate(groups):
            following = number + 1
            ahead = following < AHEAD
            if following < len(groups):
                multiply(following, 0, half, ahead)
            fill(sweep + 1, faces)
            launch(sweep + 1, faces)
            if following < len(groups):
                multiply(following, half, z_only if ahead else trace, True)
        if sweep == 0:
            pack()
        map_inputs(sweep)

    for face in range(6):
        g_v[face] = outer(mapped_v[face], packed_v[face])
    base_ref[...] = seed_v[...].astype(F32)
    inner = hid_v[:, tail:trace].astype(BF16).astype(F32)
    place = lax.broadcasted_iota(jnp.int32, (columns, LANES), 1) + tail
    base_ref[:, tail:trace] += jnp.where(place >= span, inner, 0.0)
    for pair in (Z, X):
        wait_for(sweeps - 1, pair)
        take(sweeps - 1, pair)
        for face in pair:
            given_ref[face] = dot(inp_ref[face], sel_v[face]).astype(BF16)
    wait_for(sweeps - 1, Y)
    take(sweeps - 1, Y)
    for sweep in range(sweeps):
        for face in range(6):
            @pl.when(has[face])
            def _(face=face, sweep=sweep):
                remote(sweep, face).wait_send()


def finish(
    width, base_ref, inp_ref, given_ref, sel_ref, w_ref, last_ref, g_ref,
    adjoint_hbm, gradient_hbm, adjoint_v, gradient_v, mapped_v, out_sem,
):
    columns, trace = base_ref.shape
    copies = []

    def write(source, target):
        copy = pltpu.make_async_copy(source, target, out_sem.at[len(copies)])
        copy.start()
        copies.append(copy)

    def grade(faces, mapped):
        for face in faces:
            gradient_v[face] = scaled(width, mapped[face][...], g_ref[face], last_ref[face], columns)
        part = slice(faces[0], faces[-1] + 1)
        write(gradient_v.at[part], gradient_hbm.at[part])

    for face in Y:
        mapped_v[face - Y[0]] = dot(inp_ref[face], sel_ref[face]).astype(BF16)
    grade(Z, given_ref)
    grade(X, given_ref)
    fresh = {}
    for face in range(6):
        fresh[face] = dot(inp_ref[face], w_ref[face, :, 0 : span_of(width, face)[2]])
    for low, high, faces in segments(width, 0, trace):
        value = add_faces(width, base_ref[:, low:high], fresh, low, high, faces)
        adjoint_v[:, low:high] = value.astype(BF16)
    write(adjoint_v, adjoint_hbm)
    grade(Y, [None, None, mapped_v.at[0], mapped_v.at[1]])
    for copy in copies:
        copy.wait()


def local(seed_cotangent, trace_operator, face_matrices, saved_traces, edge_flags, node_map):
    seed, operator, matrices, stored, flags, mapping = (
        array.reshape(array.shape[3:])
        for array in (
            seed_cotangent, trace_operator, face_matrices, saved_traces, edge_flags, node_map
        )
    )
    width = matrices.shape[-1]
    sweeps, columns, trace = stored.shape
    pad = up(width, LANES)
    wide = widest(width)
    anywhere = pl.BlockSpec(memory_space=pltpu.HBM)
    resident = pl.BlockSpec(memory_space=pltpu.VMEM)
    between = pl.pallas_call(
        functools.partial(exchange, width),
        out_shape=(
            jax.ShapeDtypeStruct(seed.shape, F32),
            jax.ShapeDtypeStruct((6, columns, pad), BF16),
            jax.ShapeDtypeStruct((6, columns, pad), BF16),
            jax.ShapeDtypeStruct((6, pad, pad), BF16),
            jax.ShapeDtypeStruct((6, pad, wide), BF16),
            jax.ShapeDtypeStruct((6, columns, pad), BF16),
            jax.ShapeDtypeStruct((6, pad, pad), F32),
        ),
        in_specs=[anywhere] * 6,
        out_specs=(resident,) * 7,
        scratch_shapes=[
            pltpu.VMEM(seed.shape, BF16),
            pltpu.VMEM(operator.shape, BF16),
            pltpu.VMEM(matrices.shape, BF16),
            pltpu.VMEM(stored.shape, BF16),
            pltpu.VMEM((6, 1, width), jnp.int32),
            pltpu.SMEM(flags.shape, jnp.int32),
            pltpu.VMEM((sweeps, 6, columns, pad), BF16),
            pltpu.VMEM((sweeps, 6, columns, pad), BF16),
            pltpu.VMEM((sweeps - 1, 6, columns, pad), BF16),
            pltpu.VMEM((6, (sweeps - 1) * columns, pad), BF16),
            pltpu.VMEM((6, (sweeps - 1) * columns, pad), BF16),
            pltpu.VMEM(seed.shape, F32),
            pltpu.VMEM(seed.shape, BF16),
            pltpu.VMEM((2, pad, wide), F32),
            pltpu.SemaphoreType.DMA((5,)),
            pltpu.SemaphoreType.DMA((trace // BLOCK // 2, 2)),
            pltpu.SemaphoreType.DMA((sweeps, 6)),
            pltpu.SemaphoreType.DMA((sweeps, 6)),
        ],
        compiler_params=pltpu.CompilerParams(
            collective_id=0, has_side_effects=True, vmem_limit_bytes=40 * 1024 * 1024
        ),
    )(*(pltpu.with_memory_space_constraint(array, pltpu.HBM) for array in (seed, operator, matrices, stored, mapping[:, None, :], flags)))
    adjoint, gradient = pl.pallas_call(
        functools.partial(finish, width),
        out_shape=(
            jax.ShapeDtypeStruct(seed.shape, BF16),
            jax.ShapeDtypeStruct(matrices.shape, BF16),
        ),
        in_specs=[resident] * 7,
        out_specs=(anywhere, anywhere),
        scratch_shapes=[
            pltpu.VMEM(seed.shape, BF16),
            pltpu.VMEM(matrices.shape, BF16),
            pltpu.VMEM((2, columns, pad), BF16),
            pltpu.SemaphoreType.DMA((4,)),
        ],
        compiler_params=pltpu.CompilerParams(vmem_limit_bytes=12 * 1024 * 1024),
    )(*between)
    return adjoint[None, None, None], gradient[None, None, None]


def solution(mesh):
    return jax.shard_map(
        local,
        mesh=mesh,
        in_specs=(
            P("gx", "gy", "gz", None, None),
            P("gx", "gy", "gz", None, None),
            P("gx", "gy", "gz", None, None, None),
            P("gx", "gy", "gz", None, None, None),
            P("gx", "gy", "gz", None),
            P("gx", "gy", "gz", None, None),
        ),
        out_specs=(P("gx", "gy", "gz", None, None), P("gx", "gy", "gz", None, None, None)),
        check_vma=False,
    )
```
